256 devices in a mesh: gx: 8 (over y, core), gy: 32 (over x, z).
Axes of the slice: x: 4, y: 4, z: 8, core: 2. Of those that a mesh axis runs over, the one named last changes fastest.
Arguments:
- state: float32 [4, 256, 128, 1024], P(None, 'gx', 'gy'), may hold values from -8 to 8
- diffusivity: float32 [256, 128, 1024], P('gx', 'gy'), may hold values from 0.1 to 10
Outputs:
- state_next: float32 [4, 256, 128, 1024], P(None, 'gx', 'gy')
The draws below stay inside these ranges and needn't reach their ends.
All inputs are finite; a program needn't handle non-finite values.
Results may differ from the reference program's by a relative error of at most 0.0003.
Values sent between devices are 32-bit elements; how exact they have to be, the bound alone decides.
No kernel may reach another device: no remote copies, remote signals or barrier semaphores. Data moves between devices by JAX's collectives and lax.ppermute only.
A program may use at most 64 MiB of HBM per device.

```python
import math
import jax
import jax.numpy as jnp
from jax import lax

NZ = 1024
NX = 256
NY = 128


def draw_state(key, part):
    keys = jax.random.split(jax.random.fold_in(key, 11), 2)
    rough = jax.random.normal(keys[0], (4, NX, NY, NZ), jnp.float32)
    amounts = jax.random.normal(keys[1], (4, 3, NY, NZ), jnp.float32)
    position = (jnp.arange(NX, dtype=jnp.float32) + 0.5) / NX
    orders = jnp.arange(1, 4, dtype=jnp.float32)
    modes = jnp.sin(jnp.pi * orders[:, None] * position[None, :])
    smooth = jnp.einsum('fmyz,mx->fxyz', amounts, modes)
    return jnp.clip(rough + smooth, -8.0, 8.0)


def block_scale(rng, shape, cuts, low, top_value):
    def one(dim, parts):
        heights = jax.random.uniform(jax.random.fold_in(jax.random.fold_in(rng, 6), dim), (parts,), jnp.float32, low / len(cuts), top_value / len(cuts))
        return jnp.repeat(jnp.exp(heights), shape[dim] // parts).reshape((-1,) + (1,) * (len(shape) - dim - 1))

    factor_of = one(*cuts[0])
    for cut in cuts[1:]:
        factor_of = factor_of * one(*cut)
    return factor_of


def setup_inputs(seed: int = 0) -> dict:
    arg_keys = jax.random.split(jax.random.key(seed), 3)
    return {
        "state": draw_state(jax.random.fold_in(arg_keys[2], 71), 0),
        "diffusivity": jnp.clip(jnp.exp(math.log(10.0) - 4.6051702 * jax.random.uniform(arg_keys[1], (NX, NY, NZ), jnp.float32) ** block_scale(arg_keys[1], (NX, NY, NZ), ((0, 8), (1, 32)), -0.2, 0.2)), 0.1, 10.0),
    }


diff_number = 4000.0
scalar_ratio = 1.4
step_size = 0.1


def along(field, axis):
    near = jnp.roll(field, -1, axis) - jnp.roll(field, 1, axis)
    far = jnp.roll(field, -2, axis) - jnp.roll(field, 2, axis)
    return (8.0 * near - far) / 12.0


def advect(plane):
    return -(plane[1:2] * along(plane, 1) + plane[2:3] * along(plane, 2))


def sections(plane):
    first = advect(plane)
    middle = plane + step_size * first
    return plane + 0.5 * step_size * (first + advect(middle))


def sweep(sub, main, sup, right_side):
    def down(carry, row):
        ratio_prev, value_prev = carry
        low, centre, upp, given = row
        pivot = centre - low * ratio_prev
        ratio = upp / pivot
        value = (given - low[None] * value_prev) / pivot[None]
        return (ratio, value), (ratio, value)

    start = (jnp.zeros(main.shape[1:], jnp.float32), jnp.zeros(right_side.shape[1:], jnp.float32))
    _, (ratios, values) = lax.scan(down, start, (sub, main, sup, right_side))

    def upward(after, row):
        ratio, value = row
        here = value - ratio[None] * after
        return here, here

    _, result = lax.scan(upward, jnp.zeros(right_side.shape[1:], jnp.float32), (ratios, values), reverse=True)
    return result


def line_solve(lower, upper, right_side):
    main = 1.0 + lower + upper
    zero_row = jnp.zeros_like(lower[:1])
    sub = jnp.concatenate([zero_row, -lower[1:]], 0)
    sup = jnp.concatenate([-upper[:-1], zero_row], 0)
    return sweep(sub, main, sup, right_side)


def implicit(pieces):
    rows, kappa = pieces
    zero_row = jnp.zeros_like(kappa[:1])
    padded = jnp.concatenate([zero_row, kappa, zero_row], 0)
    lower = 0.5 * diff_number * (padded[:-2] + padded[1:-1])
    upper = 0.5 * diff_number * (padded[1:-1] + padded[2:])
    flow = line_solve(lower, upper, rows[:, :3])
    heat = line_solve(scalar_ratio * lower, scalar_ratio * upper, rows[:, 3:])
    return jnp.concatenate([flow, heat], 1)


def reference(state, diffusivity):
    mixed = lax.map(sections, jnp.moveaxis(state, 1, 0))
    solved = lax.map(implicit, (jnp.moveaxis(mixed, 2, 0), jnp.moveaxis(diffusivity, 1, 0)))
    return jnp.transpose(solved, (2, 1, 0, 3))
```

```python
import functools

import jax
import jax.numpy as jnp
from jax import lax
from jax.experimental import pallas as pl
from jax.experimental.pallas import tpu as pltpu
from jax.sharding import PartitionSpec as P

diff_number = 4000.0
scalar_ratio = 1.4
step_size = 0.1


ROWS = 32
CHUNKS = (8, 8, 8, 8)
SCALES = (0.5 * diff_number, 0.5 * diff_number * scalar_ratio)
F32 = jnp.float32
VMEM = pl.BlockSpec(memory_space=pltpu.VMEM)
SMEM = pl.BlockSpec(memory_space=pltpu.SMEM)
PLANE = (32, 128)

SEG = 10
WMINE, RNEAR, RWNEAR, OMEGA, ALPHA, BETA, BETAW, MISC = 0, 2, 4, 6, 12, 14, 16, 18


def shape(*dims):
    return jax.ShapeDtypeStruct(dims, F32)


def call(kernel, outs, ins, scratch=()):
    return pl.pallas_call(
        kernel,
        out_shape=outs,
        in_specs=ins,
        out_specs=jax.tree.map(lambda _: VMEM, outs),
        scratch_shapes=list(scratch),
        compiler_params=pltpu.CompilerParams(vmem_limit_bytes=48 * 1024 * 1024),
    )


def summary_kernel(k_ref, out_ref):
    one = jnp.ones(PLANE, F32)
    zero = jnp.zeros(PLANE, F32)

    def step(i, carry):
        inv = 1.0 / (k_ref[i - 1] + k_ref[i])
        out = []
        for s in range(2):
            a, b, d, f = carry[4 * s : 4 * s + 4]
            q = inv * (1.0 / SCALES[s])
            d = q * a + d
            f = q * b + f
            out += [a + d, b + f, d, f]
        return tuple(out)

    final = lax.fori_loop(1, ROWS, step, (one, one, zero, one) * 2)
    for n in range(8):
        out_ref[n] = final[n]
    out_ref[8] = k_ref[0]
    out_ref[9] = k_ref[ROWS - 1]


def pair_kernel(pos_ref, mine_ref, other_ref, out_ref):
    right = pos_ref[0] % 2 == 1

    def lower(n):
        return jnp.where(right, other_ref[n], mine_ref[n])

    def upper(n):
        return jnp.where(right, mine_ref[n], other_ref[n])

    inv = 1.0 / (lower(9) + upper(8))
    for s in range(2):
        a, b, d, f = (lower(4 * s + n) for n in range(4))
        q = inv * (1.0 / SCALES[s])
        d = q * a + d
        f = q * b + f
        ua, ub, ud, uf = (upper(4 * s + n) for n in range(4))
        out_ref[4 * s] = ua * a + ub * d
        out_ref[4 * s + 1] = ua * b + ub * f
        out_ref[4 * s + 2] = ud * a + uf * d
        out_ref[4 * s + 3] = ud * b + uf * f
    out_ref[8] = lower(8)
    out_ref[9] = upper(9)


def coefficient_kernel(pos_ref, k_ref, mine_ref, other_ref, n1_ref, n2_ref, n3_ref, r_ref, ip_ref, wip_ref, wp_ref, misc_ref):
    position = pos_ref[0]
    right = position % 2 == 1
    chip = position // 2

    def lower(n):
        return jnp.where(right, other_ref[n], mine_ref[n])

    def upper(n):
        return jnp.where(right, mine_ref[n], other_ref[n])

    def series(scale, e, k_a, k_b):
        r = 1.0 / (1.0 + e / (scale * (k_a + k_b)))
        return r, e * r

    ahead_in, back_in = [], []
    last = []
    for s in range(2):
        scale = SCALES[s]

        def entries(get, flipped):
            a, b, d, f = (get(4 * s + n) for n in range(4))
            return (f, b, d, a) if flipped else (a, b, d, f)

        def through(get, flipped, g):
            a, b, d, f = entries(get, flipped)
            den = 1.0 / (d * g + f)
            return (a * g + b) * den, den

        def chain(far, mid, near, flipped, masks, k_own):
            tail, head = (8, 9) if flipped else (9, 8)
            e, _ = through(lambda n: far[n], flipped, scale * far[head])
            r3, g = series(scale, e, far[tail], mid[head])
            g = jnp.where(masks[2], g, scale * mid[head])
            e, den2 = through(lambda n: mid[n], flipped, g)
            r2, g = series(scale, e, mid[tail], near[head])
            g = jnp.where(masks[1], g, scale * near[head])
            e, den1 = through(lambda n: near[n], flipped, g)
            r1, g = series(scale, e, near[tail], k_own)
            g = jnp.where(masks[0], g, scale * k_own)
            w1 = jnp.where(masks[0], r1, 0.0)
            w2 = jnp.where(masks[1], r1 * r2 * den1, 0.0)
            w3 = jnp.where(masks[2], r1 * r2 * r3 * den1 * den2, 0.0)
            return g, e, (w1, w2, w3)

        left_masks = [chip >= n for n in (1, 2, 3)]
        right_masks = [chip <= n for n in (2, 1, 0)]
        g_left, _, w_left = chain(n1_ref, n2_ref, n3_ref, False, left_masks, lower(8))
        g_right, e_right, w_right = chain(n3_ref, n2_ref, n1_ref, True, right_masks, upper(9))
        e_mid, den_mid = through(lower, False, g_left)
        r_mid, g_mid = series(scale, e_mid, lower(9), upper(8))
        e_mid_b, den_mid_b = through(upper, True, g_right)
        r_mid_b, g_mid_b = series(scale, e_mid_b, lower(9), upper(8))
        _, den_upper = through(upper, False, g_mid)
        _, den_lower = through(lower, True, g_mid_b)
        misc_ref[WMINE + s] = jnp.where(right, r_mid * den_upper, r_mid_b * den_lower)
        misc_ref[RNEAR + s] = jnp.where(right, r_mid, r_mid_b)
        misc_ref[RWNEAR + s] = jnp.where(right, r_mid * den_mid, r_mid_b * den_mid_b)
        for n in range(3):
            misc_ref[OMEGA + 2 * n + s] = jnp.where(right, w_left[n], w_right[n])
        ahead_in.append(1.0 + jnp.where(right, g_mid, g_left))
        back_in.append(1.0 + jnp.where(right, g_right, g_mid_b))
        k_next = jnp.where(right, n1_ref[8], upper(8))
        inner = jnp.where(position < 7, 1.0, 0.0)
        last.append((scale * (k_ref[ROWS - 1] + k_next * inner), inner, jnp.where(right, e_right, e_mid_b)))

    one = jnp.ones(PLANE, F32)

    def step(i, carry):
        e0, e1, w0, w1, b0, b1 = carry
        j = ROWS - 1 - i
        inv = 1.0 / (k_ref[i] + k_ref[i + 1])
        inv_b = 1.0 / (k_ref[j - 1] + k_ref[j])
        out_e, out_w, out_b = [], [], []
        for s, e, w, b in ((0, e0, w0, b0), (1, e1, w1, b1)):
            q = inv * (1.0 / SCALES[s])
            r = 1.0 / (1.0 + q * e)
            ip = r * q
            r_ref[s, i] = r
            ip_ref[s, i] = ip
            wip_ref[s, i] = w * ip
            out_e.append(1.0 + e * r)
            out_w.append(w * r)
            r_b = 1.0 / (1.0 + inv_b * (1.0 / SCALES[s]) * b)
            wp_ref[s, j] = r_b
            out_b.append(1.0 + b * r_b)
        return (*out_e, *out_w, *out_b)

    carry = lax.fori_loop(0, ROWS - 1, step, (*ahead_in, one, one, *back_in))
    for s in range(2):
        e, w = carry[s], carry[2 + s]
        c, inner, e_next = last[s]
        ip = 1.0 / (c + e)
        r = c * ip
        r_ref[s, ROWS - 1] = r
        ip_ref[s, ROWS - 1] = ip
        wip_ref[s, ROWS - 1] = w * ip
        inv = 1.0 / (c + e_next)
        den = 1.0 / (e * ip + r * e_next * inv)
        beta = inner * c * inv * ip * den
        misc_ref[ALPHA + s] = inner * den / c
        misc_ref[BETA + s] = beta
        misc_ref[BETAW + s] = beta * w
        wp_ref[s, 0] = one

    def spread(i, carry):
        out = []
        for s in range(2):
            w = carry[s] * wp_ref[s, i]
            wp_ref[s, i] = w
            out.append(w)
        return tuple(out)

    lax.fori_loop(1, ROWS, spread, (one, one))


def explicit_kernel(start, count, pos_ref, left_ref, own_ref, right_ref, r_ref, wp_ref, *refs):
    if start:
        before_ref, *refs = refs
    y_ref, after_ref, mid_ref, mixed_ref = refs
    lane = lax.broadcasted_iota(jnp.int32, (8, 128), 1)
    two_low = lane < 2
    top = lane >= 127

    def along_z(q):
        w = pltpu.roll(jnp.where(two_low, pltpu.roll(q, 7, 0), q), 126, 1) - q
        g = 8.0 * w - pltpu.roll(jnp.where(top, pltpu.roll(w, 1, 0), w), 1, 1)
        return pltpu.roll(jnp.where(top, pltpu.roll(g, 1, 0), g), 1, 1) - w

    def row(c, x, j):
        if j < 0:
            return left_ref[c, x, pl.ds(j + 4, 8, stride=4), :]
        if j < 4:
            return own_ref[c, start + x, pl.ds(j, 8, stride=4), :]
        return right_ref[c, x, pl.ds(j - 4, 8, stride=4), :]

    full = step_size / 12.0

    def step(x, carry):
        speed_y = [row(1, x, j) * full for j in range(-2, 6)]
        speed_z = [row(2, x, j) * full for j in range(-2, 6)]
        for c in range(4):
            q = [row(c, x, j) for j in range(-4, 8)]
            for n in range(8):
                dy = 8.0 * (q[n + 3] - q[n + 1]) - (q[n + 4] - q[n])
                mid_ref[c, n] = q[n + 2] - (speed_y[n] * dy + speed_z[n] * along_z(q[n + 2]))
        speed_y = [mid_ref[1, n] * (0.5 * full) for n in range(2, 6)]
        speed_z = [mid_ref[2, n] * (0.5 * full) for n in range(2, 6)]
        for c in range(4):
            m = [mid_ref[c, n] for n in range(8)]
            for n in range(4):
                dy = 8.0 * (m[n + 3] - m[n + 1]) - (m[n + 4] - m[n])
                value = 0.5 * (row(c, x, n) + m[n + 2]) - (speed_y[n] * dy + speed_z[n] * along_z(m[n + 2]))
                mixed_ref[c, pl.ds(n, 8, stride=4), :] = value
        before = jnp.maximum(start + x - 1, 0)
        for c in range(4):
            s = c // 3
            f = mixed_ref[c]
            y = f + r_ref[s, before] * after_ref[0, c]
            y_ref[c, x] = y
            after_ref[0, c] = y
            after_ref[1, c] = after_ref[1, c] + wp_ref[s, start + x] * f
        return carry

    if start:
        after_ref[...] = before_ref[...]
    else:
        after_ref[...] = jnp.zeros_like(after_ref)
    lax.fori_loop(0, count, step, 0)
    if start + count == ROWS:
        right = pos_ref[0] % 2 == 1
        for c in range(4):
            ahead, back = after_ref[0, c], after_ref[1, c]
            after_ref[0, c] = jnp.where(right, back, ahead)
            after_ref[1, c] = jnp.where(right, ahead, back)


def join_kernel(pair_ref, other_ref, misc_ref, out_ref):
    for c in range(4):
        out_ref[c] = pair_ref[1, c] + misc_ref[WMINE + c // 3] * other_ref[c]


def ring_kernel(a_ref, b_ref, c_ref, misc_ref, out_ref):
    for c in range(4):
        s = c // 3
        out_ref[c] = misc_ref[OMEGA + s] * a_ref[c] + misc_ref[OMEGA + 2 + s] * b_ref[c] + misc_ref[OMEGA + 4 + s] * c_ref[c]


def final_kernel(starts, pos_ref, near_ref, own_ref, far_ref, misc_ref, r_ref, ip_ref, wip_ref, *refs):
    y_refs, (out_ref, x_ref, sem) = refs[: len(CHUNKS)], refs[len(CHUNKS) :]
    right = pos_ref[0] % 2 == 1
    inflow, after = [], []
    for c in range(4):
        s = c // 3
        near = misc_ref[RNEAR + s] * near_ref[c] + misc_ref[RWNEAR + s] * own_ref[c]
        far = far_ref[c]
        ahead = jnp.where(right, near, far)
        back = jnp.where(right, far, near)
        inflow.append(ahead)
        after.append(misc_ref[ALPHA + s] * back + misc_ref[BETA + s] * y_refs[-1][c, CHUNKS[-1] - 1] + misc_ref[BETAW + s] * ahead)

    carry = tuple(after)
    copies = []
    for n in reversed(range(len(CHUNKS))):

        def step(i, carry, n=n):
            x = CHUNKS[n] - 1 - i
            row = starts[n] + x
            out = []
            for c in range(4):
                s = c // 3
                value = y_refs[n][c, x] * ip_ref[s, row] + wip_ref[s, row] * inflow[c] + r_ref[s, row] * carry[c]
                x_ref[c, row] = value
                out.append(value)
            return tuple(out)

        carry = lax.fori_loop(0, CHUNKS[n], step, carry)
        part = pl.ds(starts[n], CHUNKS[n])
        copy = pltpu.make_async_copy(x_ref.at[:, part], out_ref.at[:, part], sem.at[n])
        copy.start()
        copies.append(copy)
    for copy in copies:
        copy.wait()


def body(state, diffusivity):
    comps, rows, ny, nz = state.shape
    tiles = nz // 128

    def natural(a):
        lead = a.shape[:-2]
        a = a.reshape(*lead, ny, tiles, 128)
        n = len(lead)
        a = jnp.transpose(a, (*range(n), n + 1, n, n + 2))
        return a.reshape(*lead, tiles * ny, 128)

    def unnatural(a):
        lead = a.shape[:-2]
        a = a.reshape(*lead, tiles, ny, 128)
        n = len(lead)
        a = jnp.transpose(a, (*range(n), n + 1, n, n + 2))
        return a.reshape(*lead, ny, nz)

    own = natural(state)
    k = natural(diffusivity)
    pos = lax.axis_index("gx").astype(jnp.int32).reshape(1)
    count = lax.axis_size("gy")
    segments = lax.axis_size("gx")
    chips = segments // 2
    starts = [sum(CHUNKS[:n]) for n in range(len(CHUNKS))]

    up = [(i, (i + 1) % count) for i in range(count)]
    down = [((i + 1) % count, i) for i in range(count)]
    lefts, rights = [], []
    for start, size in zip(starts, CHUNKS):
        piece = own[:, start : start + size]
        lefts.append(lax.ppermute(piece, "gy", up))
        rights.append(lax.ppermute(piece, "gy", down))

    pair = [(i, i ^ 1) for i in range(segments)]
    mine = call(summary_kernel, shape(SEG, *PLANE), [VMEM])(k)
    other = lax.ppermute(mine, "gx", pair)
    joined = call(pair_kernel, shape(SEG, *PLANE), [SMEM, VMEM, VMEM])(pos, mine, other)
    around = [
        lax.ppermute(joined, "gx", [((i + 2 * d) % segments, i) for i in range(segments)])
        for d in range(1, chips)
    ]
    table = shape(2, ROWS, *PLANE)
    r, ip, wip, wp, misc = call(
        coefficient_kernel,
        (table, table, table, table, shape(MISC, *PLANE)),
        [SMEM] + [VMEM] * 6,
    )(pos, k, mine, other, *around)

    ys = []
    carry = ()
    for n, (start, size) in enumerate(zip(starts, CHUNKS)):
        y, after = call(
            functools.partial(explicit_kernel, start, size),
            (shape(comps, size, *PLANE), shape(2, comps, *PLANE)),
            [SMEM] + [VMEM] * (5 + len(carry)),
            [pltpu.VMEM((comps, 8, 8, 128), F32), pltpu.VMEM((comps, *PLANE), F32)],
        )(pos, lefts[n], own, rights[n], r, wp, *carry)
        carry = (after,)
        ys.append(y)

    near = lax.ppermute(after[0], "gx", pair)
    plane = shape(comps, *PLANE)
    out_flow = call(join_kernel, plane, [VMEM] * 3)(after, near, misc)
    flows = []
    for d in range(1, chips):
        ways = [(2 * i + 1, 2 * (i + d) + 1) for i in range(chips - d)]
        ways += [(2 * (i + d), 2 * i) for i in range(chips - d)]
        flows.append(lax.ppermute(out_flow, "gx", ways))
    in_flow = call(ring_kernel, plane, [VMEM] * 4)(*flows, misc)
    far = lax.ppermute(in_flow, "gx", pair)
    result = pl.pallas_call(
        functools.partial(final_kernel, starts),
        out_shape=shape(comps, rows, *PLANE),
        in_specs=[SMEM] + [VMEM] * (7 + len(ys)),
        out_specs=pl.BlockSpec(memory_space=pl.ANY),
        scratch_shapes=[
            pltpu.VMEM((comps, rows, *PLANE), F32),
            pltpu.SemaphoreType.DMA((len(CHUNKS),)),
        ],
        compiler_params=pltpu.CompilerParams(vmem_limit_bytes=48 * 1024 * 1024),
    )(pos, near, in_flow, far, misc, r, ip, wip, *ys)
    return unnatural(result)


def solution(mesh):
    return jax.shard_map(
        body,
        mesh=mesh,
        in_specs=(P(None, "gx", "gy", None), P("gx", "gy", None)),
        out_specs=P(None, "gx", "gy", None),
        check_vma=False,
    )
```

```python
import functools

import jax
import jax.numpy as jnp
from jax import lax
from jax.experimental import pallas as pl
from jax.experimental.pallas import tpu as pltpu
from jax.sharding import PartitionSpec as P

diff_number = 4000.0
scalar_ratio = 1.4
step_size = 0.1


ROWS = 32
CHUNKS = (17, 9, 4, 2)
FIRST_ROOM = 63672 * 1024
PIECE = 6
SCALES = (0.5 * diff_number, 0.5 * diff_number * scalar_ratio)
F32 = jnp.float32
VMEM = pl.BlockSpec(memory_space=pltpu.VMEM)
SMEM = pl.BlockSpec(memory_space=pltpu.SMEM)
PLANE = (32, 128)

SEG = 10
(W_UP, W_DOWN, R_UP, R_DOWN, RW_UP, RW_DOWN, AHEAD, _, _, BACK, _, _, ALPHA, BETA, BETAW) = range(0, 30, 2)
MISC = 30


def shape(*dims):
    return jax.ShapeDtypeStruct(dims, F32)


def call(kernel, outs, ins, scratch=(), room=16 * 1024 * 1024):
    return pl.pallas_call(
        kernel,
        out_shape=outs,
        in_specs=ins,
        out_specs=jax.tree.map(lambda _: VMEM, outs),
        scratch_shapes=list(scratch),
        compiler_params=pltpu.CompilerParams(vmem_limit_bytes=room),
    )


def summary_kernel(k_ref, out_ref):
    one = jnp.ones(PLANE, F32)
    zero = jnp.zeros(PLANE, F32)

    def step(i, carry):
        inv = 1.0 / (k_ref[i - 1] + k_ref[i])
        out = []
        for s in range(2):
            a, b, d, f = carry[4 * s : 4 * s + 4]
            q = inv * (1.0 / SCALES[s])
            d = q * a + d
            f = q * b + f
            out += [a + d, b + f, d, f]
        return tuple(out)

    final = lax.fori_loop(1, ROWS, step, (one, one, zero, one) * 2)
    for n in range(8):
        out_ref[n] = final[n]
    out_ref[8] = k_ref[0]
    out_ref[9] = k_ref[ROWS - 1]


def pair_kernel(pos_ref, mine_ref, other_ref, out_ref):
    right = pos_ref[0] % 2 == 1

    def lower(n):
        return jnp.where(right, other_ref[n], mine_ref[n])

    def upper(n):
        return jnp.where(right, mine_ref[n], other_ref[n])

    inv = 1.0 / (lower(9) + upper(8))
    for s in range(2):
        a, b, d, f = (lower(4 * s + n) for n in range(4))
        q = inv * (1.0 / SCALES[s])
        d = q * a + d
        f = q * b + f
        ua, ub, ud, uf = (upper(4 * s + n) for n in range(4))
        out_ref[4 * s] = ua * a + ub * d
        out_ref[4 * s + 1] = ua * b + ub * f
        out_ref[4 * s + 2] = ud * a + uf * d
        out_ref[4 * s + 3] = ud * b + uf * f
    out_ref[8] = lower(8)
    out_ref[9] = upper(9)


def coefficient_kernel(pos_ref, k_ref, mine_ref, other_ref, n1_ref, n2_ref, n3_ref, r_ref, ip_ref, wip_ref, wp_ref, misc_ref):
    position = pos_ref[0]
    right = position % 2 == 1
    chip = position // 2

    def lower(n):
        return jnp.where(right, other_ref[n], mine_ref[n])

    def upper(n):
        return jnp.where(right, mine_ref[n], other_ref[n])

    def series(scale, e, k_a, k_b):
        r = 1.0 / (1.0 + e / (scale * (k_a + k_b)))
        return r, e * r

    ahead_in, back_in = [], []
    last = []
    for s in range(2):
        scale = SCALES[s]

        def entries(get, flipped):
            a, b, d, f = (get(4 * s + n) for n in range(4))
            return (f, b, d, a) if flipped else (a, b, d, f)

        def through(get, flipped, g):
            a, b, d, f = entries(get, flipped)
            den = 1.0 / (d * g + f)
            return (a * g + b) * den, den

        def chain(far, mid, near, flipped, masks, k_own):
            tail, head = (8, 9) if flipped else (9, 8)
            e, _ = through(lambda n: far[n], flipped, scale * far[head])
            r3, g = series(scale, e, far[tail], mid[head])
            g = jnp.where(masks[2], g, scale * mid[head])
            e, den2 = through(lambda n: mid[n], flipped, g)
            r2, g = series(scale, e, mid[tail], near[head])
            g = jnp.where(masks[1], g, scale * near[head])
            e, den1 = through(lambda n: near[n], flipped, g)
            r1, g = series(scale, e, near[tail], k_own)
            g = jnp.where(masks[0], g, scale * k_own)
            w1 = jnp.where(masks[0], r1, 0.0)
            w2 = jnp.where(masks[1], r1 * r2 * den1, 0.0)
            w3 = jnp.where(masks[2], r1 * r2 * r3 * den1 * den2, 0.0)
            return g, e, (w1, w2, w3)

        left_masks = [chip >= n for n in (1, 2, 3)]
        right_masks = [chip <= n for n in (2, 1, 0)]
        g_left, _, ahead = chain(n1_ref, n2_ref, n3_ref, False, left_masks, lower(8))
        g_right, e_right, back = chain(n3_ref, n2_ref, n1_ref, True, right_masks, upper(9))
        e_mid, den_mid = through(lower, False, g_left)
        r_mid, g_mid = series(scale, e_mid, lower(9), upper(8))
        e_mid_b, den_mid_b = through(upper, True, g_right)
        r_mid_b, g_mid_b = series(scale, e_mid_b, lower(9), upper(8))
        _, den_upper = through(upper, False, g_mid)
        _, den_lower = through(lower, True, g_mid_b)
        misc_ref[W_UP + s] = r_mid * den_upper
        misc_ref[W_DOWN + s] = r_mid_b * den_lower
        misc_ref[R_UP + s] = r_mid
        misc_ref[R_DOWN + s] = r_mid_b
        misc_ref[RW_UP + s] = r_mid * den_mid
        misc_ref[RW_DOWN + s] = r_mid_b * den_mid_b
        for n in range(3):
            misc_ref[AHEAD + 2 * n + s] = ahead[n]
            misc_ref[BACK + 2 * n + s] = back[2 - n]
        ahead_in.append(1.0 + jnp.where(right, g_mid, g_left))
        back_in.append(1.0 + jnp.where(right, g_right, g_mid_b))
        k_next = jnp.where(right, n1_ref[8], upper(8))
        inner = jnp.where(position < 7, 1.0, 0.0)
        last.append((scale * (k_ref[ROWS - 1] + k_next * inner), inner, jnp.where(right, e_right, e_mid_b)))

    one = jnp.ones(PLANE, F32)

    def step(i, carry):
        e0, e1, w0, w1, b0, b1 = carry
        j = ROWS - 1 - i
        inv = 1.0 / (k_ref[i] + k_ref[i + 1])
        inv_b = 1.0 / (k_ref[j - 1] + k_ref[j])
        out_e, out_w, out_b = [], [], []
        for s, e, w, b in ((0, e0, w0, b0), (1, e1, w1, b1)):
            q = inv * (1.0 / SCALES[s])
            r = 1.0 / (1.0 + q * e)
            ip = r * q
            r_ref[s, i] = r
            ip_ref[s, i] = ip
            wip_ref[s, i] = w * ip
            out_e.append(1.0 + e * r)
            out_w.append(w * r)
            r_b = 1.0 / (1.0 + inv_b * (1.0 / SCALES[s]) * b)
            wp_ref[s, j] = r_b
            out_b.append(1.0 + b * r_b)
        return (*out_e, *out_w, *out_b)

    carry = lax.fori_loop(0, ROWS - 1, step, (*ahead_in, one, one, *back_in))
    for s in range(2):
        e, w = carry[s], carry[2 + s]
        c, inner, e_next = last[s]
        ip = 1.0 / (c + e)
        r = c * ip
        r_ref[s, ROWS - 1] = r
        ip_ref[s, ROWS - 1] = ip
        wip_ref[s, ROWS - 1] = w * ip
        inv = 1.0 / (c + e_next)
        den = 1.0 / (e * ip + r * e_next * inv)
        beta = inner * c * inv * ip * den
        misc_ref[ALPHA + s] = inner * den / c
        misc_ref[BETA + s] = beta
        misc_ref[BETAW + s] = beta * w
        wp_ref[s, 0] = one

    def spread(i, carry):
        out = []
        for s in range(2):
            w = carry[s] * wp_ref[s, i]
            wp_ref[s, i] = w
            out.append(w)
        return tuple(out)

    lax.fori_loop(1, ROWS, spread, (one, one))


def explicit_kernel(start, count, left_ref, own_ref, right_ref, r_ref, wp_ref, *refs):
    if start:
        before_ref, *refs = refs
    y_ref, after_ref, mid_ref, mixed_ref = refs
    lane = lax.broadcasted_iota(jnp.int32, (8, 128), 1)
    two_low = lane < 2
    top = lane >= 127

    def along_z(q):
        w = pltpu.roll(jnp.where(two_low, pltpu.roll(q, 7, 0), q), 126, 1) - q
        g = 8.0 * w - pltpu.roll(jnp.where(top, pltpu.roll(w, 1, 0), w), 1, 1)
        return pltpu.roll(jnp.where(top, pltpu.roll(g, 1, 0), g), 1, 1) - w

    def row(c, x, j):
        if j < 0:
            return left_ref[c, x, pl.ds(j + 4, 8, stride=4), :]
        if j < 4:
            return own_ref[c, start + x, pl.ds(j, 8, stride=4), :]
        return right_ref[c, x, pl.ds(j - 4, 8, stride=4), :]

    full = step_size / 12.0

    def step(x, carry):
        speed_y = [row(1, x, j) * full for j in range(-2, 6)]
        speed_z = [row(2, x, j) * full for j in range(-2, 6)]
        for c in range(4):
            q = [row(c, x, j) for j in range(-4, 8)]
            for n in range(8):
                dy = 8.0 * (q[n + 3] - q[n + 1]) - (q[n + 4] - q[n])
                mid_ref[c, n] = q[n + 2] - (speed_y[n] * dy + speed_z[n] * along_z(q[n + 2]))
        speed_y = [mid_ref[1, n] * (0.5 * full) for n in range(2, 6)]
        speed_z = [mid_ref[2, n] * (0.5 * full) for n in range(2, 6)]
        for c in range(4):
            m = [mid_ref[c, n] for n in range(8)]
            for n in range(4):
                dy = 8.0 * (m[n + 3] - m[n + 1]) - (m[n + 4] - m[n])
                value = 0.5 * (row(c, x, n) + m[n + 2]) - (speed_y[n] * dy + speed_z[n] * along_z(m[n + 2]))
                mixed_ref[c, pl.ds(n, 8, stride=4), :] = value
        before = jnp.maximum(start + x - 1, 0)
        for c in range(4):
            s = c // 3
            f = mixed_ref[c]
            y = f + r_ref[s, before] * after_ref[0, c]
            y_ref[c, x] = y
            after_ref[0, c] = y
            after_ref[1, c] = after_ref[1, c] + wp_ref[s, start + x] * f
        return carry

    if start:
        after_ref[...] = before_ref[...]
    else:
        after_ref[...] = jnp.zeros_like(after_ref)
    lax.fori_loop(0, count, step, 0)


def chip_kernel(pos_ref, own_ref, lower_ref, misc_ref, *out_refs):
    chip = pos_ref[0] // 2
    for c in range(4):
        s = c // 3
        ahead = own_ref[0, c] + misc_ref[W_UP + s] * lower_ref[0, c]
        back = lower_ref[1, c] + misc_ref[W_DOWN + s] * own_ref[1, c]
        for d, out_ref in enumerate(out_refs, 1):
            out_ref[c] = jnp.where(chip + d < 4, ahead, back)


def inflow_kernel(own_ref, lower_ref, a_ref, b_ref, c_ref, misc_ref, away_ref, here_ref):
    for c in range(4):
        s = c // 3
        values = a_ref[c], b_ref[c], c_ref[c]
        ahead = sum(misc_ref[AHEAD + 2 * n + s] * values[n] for n in range(3))
        back = sum(misc_ref[BACK + 2 * n + s] * values[n] for n in range(3))
        away_ref[0, c] = ahead
        away_ref[1, c] = misc_ref[R_DOWN + s] * own_ref[1, c] + misc_ref[RW_DOWN + s] * back
        here_ref[0, c] = misc_ref[R_UP + s] * lower_ref[0, c] + misc_ref[RW_UP + s] * ahead
        here_ref[1, c] = back


def final_kernel(starts, pieces, pos_ref, lower_ref, upper_ref, misc_ref, r_ref, ip_ref, wip_ref, *refs):
    y_refs, (out_ref, x_ref, sem) = refs[: len(CHUNKS)], refs[len(CHUNKS) :]
    right = pos_ref[0] % 2 == 1
    inflow, after = [], []
    for c in range(4):
        s = c // 3
        ahead = jnp.where(right, upper_ref[0, c], lower_ref[0, c])
        back = jnp.where(right, upper_ref[1, c], lower_ref[1, c])
        inflow.append(ahead)
        after.append(misc_ref[ALPHA + s] * back + misc_ref[BETA + s] * y_refs[-1][c, CHUNKS[-1] - 1] + misc_ref[BETAW + s] * ahead)

    carry = tuple(after)
    copies = []
    for number, (n, low, high) in enumerate(pieces):

        def step(i, carry, n=n, high=high):
            x = high - 1 - i
            row = starts[n] + x
            out = []
            for c in range(4):
                s = c // 3
                value = y_refs[n][c, x] * ip_ref[s, row] + wip_ref[s, row] * inflow[c] + r_ref[s, row] * carry[c]
                x_ref[c, row] = value
                out.append(value)
            return tuple(out)

        carry = lax.fori_loop(0, high - low, step, carry)
        part = pl.ds(starts[n] + low, high - low)
        copy = pltpu.make_async_copy(x_ref.at[:, part], out_ref.at[:, part], sem.at[number])
        copy.start()
        copies.append(copy)
    for copy in copies:
        copy.wait()


def cut_kernel(start, count, whole_ref, *refs):
    out_ref, sem = refs[-2:]
    copy = pltpu.make_async_copy(whole_ref.at[:, pl.ds(start, count)], out_ref, sem)
    copy.start()
    copy.wait()


def body(state, diffusivity):
    comps, rows, ny, nz = state.shape
    tiles = nz // 128

    def natural(a):
        lead = a.shape[:-2]
        a = a.reshape(*lead, ny, tiles, 128)
        n = len(lead)
        a = jnp.transpose(a, (*range(n), n + 1, n, n + 2))
        return a.reshape(*lead, tiles * ny, 128)

    def unnatural(a):
        lead = a.shape[:-2]
        a = a.reshape(*lead, tiles, ny, 128)
        n = len(lead)
        a = jnp.transpose(a, (*range(n), n + 1, n, n + 2))
        return a.reshape(*lead, ny, nz)

    own = natural(state)
    k = natural(diffusivity)
    pos = lax.axis_index("gx").astype(jnp.int32).reshape(1)
    count = lax.axis_size("gy")
    segments = lax.axis_size("gx")
    chips = segments // 2
    starts = [sum(CHUNKS[:n]) for n in range(len(CHUNKS))]

    anywhere = pl.BlockSpec(memory_space=pl.ANY)
    hbm = pl.BlockSpec(memory_space=pltpu.HBM)
    up = [(i, (i + 1) % count) for i in range(count)]
    down = [((i + 1) % count, i) for i in range(count)]
    lefts, rights = [], []

    def send(n, *behind):
        piece = call(
            functools.partial(cut_kernel, starts[n], CHUNKS[n]),
            shape(comps, CHUNKS[n], *PLANE),
            [hbm] + [anywhere] * len(behind),
            [pltpu.SemaphoreType.DMA(())],
            16 * 1024 * 1024 if n else FIRST_ROOM,
        )(own, *behind)
        lefts.append(lax.ppermute(piece, "gy", up))
        rights.append(lax.ppermute(piece, "gy", down))

    send(0)
    pair = [(i, i ^ 1) for i in range(segments)]
    mine = call(summary_kernel, shape(SEG, *PLANE), [VMEM])(k)
    other = lax.ppermute(mine, "gx", pair)
    joined = call(pair_kernel, shape(SEG, *PLANE), [SMEM, VMEM, VMEM])(pos, mine, other)
    for n in range(1, len(CHUNKS)):
        send(n, joined)
    around = [
        lax.ppermute(joined, "gx", [((i + 2 * d) % segments, i) for i in range(segments)])
        for d in range(1, chips)
    ]
    table = shape(2, ROWS, *PLANE)
    r, ip, wip, wp, misc = call(
        coefficient_kernel,
        (table, table, table, table, shape(MISC, *PLANE)),
        [SMEM] + [VMEM] * 6,
    )(pos, k, mine, other, *around)

    ys = []
    carry = ()
    both = shape(2, comps, *PLANE)
    for n, (start, size) in enumerate(zip(starts, CHUNKS)):
        y, ends = call(
            functools.partial(explicit_kernel, start, size),
            (shape(comps, size, *PLANE), both),
            [VMEM] * (5 + len(carry)),
            [pltpu.VMEM((comps, 8, 8, 128), F32), pltpu.VMEM((comps, *PLANE), F32)],
        )(lefts[n], own, rights[n], r, wp, *carry)
        carry = (ends,)
        ys.append(y)

    lower_ends = lax.ppermute(ends, "gx", pair)
    plane = shape(comps, *PLANE)
    chip_ends = call(chip_kernel, (plane,) * (chips - 1), [SMEM] + [VMEM] * 3)(pos, ends, lower_ends, misc)
    flows = []
    for d in range(1, chips):
        ways = []
        for i in range(segments):
            for j in range(count):
                to = ((i + 2 * d) % segments, j) if i % 2 else (i, j ^ 8)
                ways.append((i * count + j, to[0] * count + to[1]))
        flows.append(lax.ppermute(chip_ends[d - 1], ("gx", "gy"), ways))
    away, here = call(inflow_kernel, (both, both), [VMEM] * 6)(ends, lower_ends, *flows, misc)
    from_upper = lax.ppermute(away, "gx", pair)
    pieces = []
    for n in reversed(range(len(CHUNKS))):
        for high in range(CHUNKS[n], 0, -PIECE):
            pieces.append((n, max(high - PIECE, 0), high))
    result = pl.pallas_call(
        functools.partial(final_kernel, starts, pieces),
        out_shape=shape(comps, rows, *PLANE),
        in_specs=[SMEM] + [VMEM] * (6 + len(ys)),
        out_specs=anywhere,
        scratch_shapes=[
            pltpu.VMEM((comps, rows, *PLANE), F32),
            pltpu.SemaphoreType.DMA((len(pieces),)),
        ],
        compiler_params=pltpu.CompilerParams(vmem_limit_bytes=16 * 1024 * 1024),
    )(pos, from_upper, here, misc, r, ip, wip, *ys)
    return unnatural(result)


def solution(mesh):
    return jax.shard_map(
        body,
        mesh=mesh,
        in_specs=(P(None, "gx", "gy", None), P("gx", "gy", None)),
        out_specs=P(None, "gx", "gy", None),
        check_vma=False,
    )
```

```python
import functools

import jax
import jax.numpy as jnp
from jax import lax
from jax.experimental import pallas as pl
from jax.experimental.pallas import tpu as pltpu
from jax.sharding import PartitionSpec as P

diff_number = 4000.0
scalar_ratio = 1.4
step_size = 0.1


ROWS = 32
CHUNKS = (17, 9, 4, 2)
FIRST_ROOM = 63672 * 1024
PIECE = 6
SCALES = (0.5 * diff_number, 0.5 * diff_number * scalar_ratio)
F32 = jnp.float32
VMEM = pl.BlockSpec(memory_space=pltpu.VMEM)
SMEM = pl.BlockSpec(memory_space=pltpu.SMEM)
PLANE = (32, 128)

SEG = 10
(W_UP, W_DOWN, R_UP, R_DOWN, RW_UP, RW_DOWN, AHEAD, _, _, BACK, _, _, ALPHA, BETA, BETAW) = range(0, 30, 2)
MISC = 30


def shape(*dims):
    return jax.ShapeDtypeStruct(dims, F32)


def call(kernel, outs, ins, scratch=(), room=16 * 1024 * 1024):
    return pl.pallas_call(
        kernel,
        out_shape=outs,
        in_specs=ins,
        out_specs=jax.tree.map(lambda _: VMEM, outs),
        scratch_shapes=list(scratch),
        compiler_params=pltpu.CompilerParams(vmem_limit_bytes=room),
    )


def summary_kernel(k_ref, out_ref):
    one = jnp.ones(PLANE, F32)
    zero = jnp.zeros(PLANE, F32)

    def step(i, carry):
        inv = 1.0 / (k_ref[i - 1] + k_ref[i])
        out = []
        for s in range(2):
            a, b, d, f = carry[4 * s : 4 * s + 4]
            q = inv * (1.0 / SCALES[s])
            d = q * a + d
            f = q * b + f
            out += [a + d, b + f, d, f]
        return tuple(out)

    final = lax.fori_loop(1, ROWS, step, (one, one, zero, one) * 2)
    for n in range(8):
        out_ref[n] = final[n]
    out_ref[8] = k_ref[0]
    out_ref[9] = k_ref[ROWS - 1]


def pair_kernel(pos_ref, mine_ref, other_ref, out_ref):
    right = pos_ref[0] % 2 == 1

    def lower(n):
        return jnp.where(right, other_ref[n], mine_ref[n])

    def upper(n):
        return jnp.where(right, mine_ref[n], other_ref[n])

    inv = 1.0 / (lower(9) + upper(8))
    for s in range(2):
        a, b, d, f = (lower(4 * s + n) for n in range(4))
        q = inv * (1.0 / SCALES[s])
        d = q * a + d
        f = q * b + f
        ua, ub, ud, uf = (upper(4 * s + n) for n in range(4))
        out_ref[4 * s] = ua * a + ub * d
        out_ref[4 * s + 1] = ua * b + ub * f
        out_ref[4 * s + 2] = ud * a + uf * d
        out_ref[4 * s + 3] = ud * b + uf * f
    out_ref[8] = lower(8)
    out_ref[9] = upper(9)


def coefficient_kernel(pos_ref, k_ref, mine_ref, other_ref, n1_ref, n2_ref, n3_ref, r_ref, ip_ref, wip_ref, wp_ref, misc_ref):
    position = pos_ref[0]
    right = position % 2 == 1
    chip = position // 2

    def lower(n):
        return jnp.where(right, other_ref[n], mine_ref[n])

    def upper(n):
        return jnp.where(right, mine_ref[n], other_ref[n])

    def series(scale, e, k_a, k_b):
        r = 1.0 / (1.0 + e / (scale * (k_a + k_b)))
        return r, e * r

    ahead_in, back_in = [], []
    last = []
    for s in range(2):
        scale = SCALES[s]

        def entries(get, flipped):
            a, b, d, f = (get(4 * s + n) for n in range(4))
            return (f, b, d, a) if flipped else (a, b, d, f)

        def through(get, flipped, g):
            a, b, d, f = entries(get, flipped)
            den = 1.0 / (d * g + f)
            return (a * g + b) * den, den

        def chain(far, mid, near, flipped, masks, k_own):
            tail, head = (8, 9) if flipped else (9, 8)
            e, _ = through(lambda n: far[n], flipped, scale * far[head])
            r3, g = series(scale, e, far[tail], mid[head])
            g = jnp.where(masks[2], g, scale * mid[head])
            e, den2 = through(lambda n: mid[n], flipped, g)
            r2, g = series(scale, e, mid[tail], near[head])
            g = jnp.where(masks[1], g, scale * near[head])
            e, den1 = through(lambda n: near[n], flipped, g)
            r1, g = series(scale, e, near[tail], k_own)
            g = jnp.where(masks[0], g, scale * k_own)
            w1 = jnp.where(masks[0], r1, 0.0)
            w2 = jnp.where(masks[1], r1 * r2 * den1, 0.0)
            w3 = jnp.where(masks[2], r1 * r2 * r3 * den1 * den2, 0.0)
            return g, e, (w1, w2, w3)

        left_masks = [chip >= n for n in (1, 2, 3)]
        right_masks = [chip <= n for n in (2, 1, 0)]
        g_left, _, ahead = chain(n1_ref, n2_ref, n3_ref, False, left_masks, lower(8))
        g_right, e_right, back = chain(n3_ref, n2_ref, n1_ref, True, right_masks, upper(9))
        e_mid, den_mid = through(lower, False, g_left)
        r_mid, g_mid = series(scale, e_mid, lower(9), upper(8))
        e_mid_b, den_mid_b = through(upper, True, g_right)
        r_mid_b, g_mid_b = series(scale, e_mid_b, lower(9), upper(8))
        _, den_upper = through(upper, False, g_mid)
        _, den_lower = through(lower, True, g_mid_b)
        misc_ref[W_UP + s] = r_mid * den_upper
        misc_ref[W_DOWN + s] = r_mid_b * den_lower
        misc_ref[R_UP + s] = r_mid
        misc_ref[R_DOWN + s] = r_mid_b
        misc_ref[RW_UP + s] = r_mid * den_mid
        misc_ref[RW_DOWN + s] = r_mid_b * den_mid_b
        for n in range(3):
            misc_ref[AHEAD + 2 * n + s] = ahead[n]
            misc_ref[BACK + 2 * n + s] = back[2 - n]
        ahead_in.append(1.0 + jnp.where(right, g_mid, g_left))
        back_in.append(1.0 + jnp.where(right, g_right, g_mid_b))
        k_next = jnp.where(right, n1_ref[8], upper(8))
        inner = jnp.where(position < 7, 1.0, 0.0)
        last.append((scale * (k_ref[ROWS - 1] + k_next * inner), inner, jnp.where(right, e_right, e_mid_b)))

    one = jnp.ones(PLANE, F32)

    def step(i, carry):
        e0, e1, w0, w1, b0, b1 = carry
        j = ROWS - 1 - i
        inv = 1.0 / (k_ref[i] + k_ref[i + 1])
        inv_b = 1.0 / (k_ref[j - 1] + k_ref[j])
        out_e, out_w, out_b = [], [], []
        for s, e, w, b in ((0, e0, w0, b0), (1, e1, w1, b1)):
            q = inv * (1.0 / SCALES[s])
            r = 1.0 / (1.0 + q * e)
            ip = r * q
            r_ref[s, i] = r
            ip_ref[s, i] = ip
            wip_ref[s, i] = w * ip
            out_e.append(1.0 + e * r)
            out_w.append(w * r)
            r_b = 1.0 / (1.0 + inv_b * (1.0 / SCALES[s]) * b)
            wp_ref[s, j] = r_b
            out_b.append(1.0 + b * r_b)
        return (*out_e, *out_w, *out_b)

    carry = lax.fori_loop(0, ROWS - 1, step, (*ahead_in, one, one, *back_in))
    for s in range(2):
        e, w = carry[s], carry[2 + s]
        c, inner, e_next = last[s]
        ip = 1.0 / (c + e)
        r = c * ip
        r_ref[s, ROWS - 1] = r
        ip_ref[s, ROWS - 1] = ip
        wip_ref[s, ROWS - 1] = w * ip
        inv = 1.0 / (c + e_next)
        den = 1.0 / (e * ip + r * e_next * inv)
        beta = inner * c * inv * ip * den
        misc_ref[ALPHA + s] = inner * den / c
        misc_ref[BETA + s] = beta
        misc_ref[BETAW + s] = beta * w
        wp_ref[s, 0] = one

    def spread(i, carry):
        out = []
        for s in range(2):
            w = carry[s] * wp_ref[s, i]
            wp_ref[s, i] = w
            out.append(w)
        return tuple(out)

    lax.fori_loop(1, ROWS, spread, (one, one))


def explicit_kernel(start, count, left_ref, own_ref, right_ref, r_ref, wp_ref, *refs):
    if start:
        before_ref, *refs = refs
    y_ref, after_ref, mid_ref, mixed_ref = refs
    lane = lax.broadcasted_iota(jnp.int32, (8, 128), 1)
    two_low = lane < 2
    top = lane >= 127

    def along_z(q):
        w = pltpu.roll(jnp.where(two_low, pltpu.roll(q, 7, 0), q), 126, 1) - q
        g = 8.0 * w - pltpu.roll(jnp.where(top, pltpu.roll(w, 1, 0), w), 1, 1)
        return pltpu.roll(jnp.where(top, pltpu.roll(g, 1, 0), g), 1, 1) - w

    def row(c, x, j):
        if j < 0:
            return left_ref[c, x, pl.ds(j + 4, 8, stride=4), :]
        if j < 4:
            return own_ref[c, start + x, pl.ds(j, 8, stride=4), :]
        return right_ref[c, x, pl.ds(j - 4, 8, stride=4), :]

    full = step_size / 12.0

    def step(x, carry):
        speed_y = [row(1, x, j) * full for j in range(-2, 6)]
        speed_z = [row(2, x, j) * full for j in range(-2, 6)]
        for c in range(4):
            q = [row(c, x, j) for j in range(-4, 8)]
            for n in range(8):
                dy = 8.0 * (q[n + 3] - q[n + 1]) - (q[n + 4] - q[n])
                mid_ref[c, n] = q[n + 2] - (speed_y[n] * dy + speed_z[n] * along_z(q[n + 2]))
        speed_y = [mid_ref[1, n] * (0.5 * full) for n in range(2, 6)]
        speed_z = [mid_ref[2, n] * (0.5 * full) for n in range(2, 6)]
        for c in range(4):
            m = [mid_ref[c, n] for n in range(8)]
            for n in range(4):
                dy = 8.0 * (m[n + 3] - m[n + 1]) - (m[n + 4] - m[n])
                value = 0.5 * (row(c, x, n) + m[n + 2]) - (speed_y[n] * dy + speed_z[n] * along_z(m[n + 2]))
                mixed_ref[c, pl.ds(n, 8, stride=4), :] = value
        before = jnp.maximum(start + x - 1, 0)
        for c in range(4):
            s = c // 3
            f = mixed_ref[c]
            y = f + r_ref[s, before] * after_ref[0, c]
            y_ref[c, x] = y
            after_ref[0, c] = y
            after_ref[1, c] = after_ref[1, c] + wp_ref[s, start + x] * f
        return carry

    if start:
        after_ref[...] = before_ref[...]
    else:
        after_ref[...] = jnp.zeros_like(after_ref)
    lax.fori_loop(0, count, step, 0)


def chip_kernel(pos_ref, own_ref, other_ref, misc_ref, *out_refs):
    right = pos_ref[0] % 2 == 1
    chip = pos_ref[0] // 2
    for c in range(4):
        s = c // 3
        own, other = (own_ref[0, c], own_ref[1, c]), (other_ref[0, c], other_ref[1, c])
        lower = [jnp.where(right, o, m) for m, o in zip(own, other)]
        upper = [jnp.where(right, m, o) for m, o in zip(own, other)]
        ahead = upper[0] + misc_ref[W_UP + s] * lower[0]
        back = lower[1] + misc_ref[W_DOWN + s] * upper[1]
        for d, out_ref in enumerate(out_refs, 1):
            out_ref[c] = jnp.where(chip + d < 4, ahead, back)


def final_kernel(starts, pieces, pos_ref, other_ref, a_ref, b_ref, c_ref, misc_ref, r_ref, ip_ref, wip_ref, *refs):
    y_refs, (out_ref, x_ref, sem) = refs[: len(CHUNKS)], refs[len(CHUNKS) :]
    right = pos_ref[0] % 2 == 1
    inflow, after = [], []
    for c in range(4):
        s = c // 3
        values = a_ref[c], b_ref[c], c_ref[c]
        ahead = sum(misc_ref[AHEAD + 2 * n + s] * values[n] for n in range(3))
        back = sum(misc_ref[BACK + 2 * n + s] * values[n] for n in range(3))
        near_ahead = misc_ref[R_UP + s] * other_ref[0, c] + misc_ref[RW_UP + s] * ahead
        near_back = misc_ref[R_DOWN + s] * other_ref[1, c] + misc_ref[RW_DOWN + s] * back
        ahead, back = jnp.where(right, near_ahead, ahead), jnp.where(right, back, near_back)
        inflow.append(ahead)
        after.append(misc_ref[ALPHA + s] * back + misc_ref[BETA + s] * y_refs[-1][c, CHUNKS[-1] - 1] + misc_ref[BETAW + s] * ahead)

    carry = tuple(after)
    copies = []
    for number, (n, low, high) in enumerate(pieces):

        def step(i, carry, n=n, high=high):
            x = high - 1 - i
            row = starts[n] + x
            out = []
            for c in range(4):
                s = c // 3
                value = y_refs[n][c, x] * ip_ref[s, row] + wip_ref[s, row] * inflow[c] + r_ref[s, row] * carry[c]
                x_ref[c, row] = value
                out.append(value)
            return tuple(out)

        carry = lax.fori_loop(0, high - low, step, carry)
        part = pl.ds(starts[n] + low, high - low)
        copy = pltpu.make_async_copy(x_ref.at[:, part], out_ref.at[:, part], sem.at[number])
        copy.start()
        copies.append(copy)
    for copy in copies:
        copy.wait()


def cut_kernel(start, count, whole_ref, *refs):
    out_ref, sem = refs[-2:]
    copy = pltpu.make_async_copy(whole_ref.at[:, pl.ds(start, count)], out_ref, sem)
    copy.start()
    copy.wait()


def body(state, diffusivity):
    comps, rows, ny, nz = state.shape
    tiles = nz // 128

    def natural(a):
        lead = a.shape[:-2]
        a = a.reshape(*lead, ny, tiles, 128)
        n = len(lead)
        a = jnp.transpose(a, (*range(n), n + 1, n, n + 2))
        return a.reshape(*lead, tiles * ny, 128)

    def unnatural(a):
        lead = a.shape[:-2]
        a = a.reshape(*lead, tiles, ny, 128)
        n = len(lead)
        a = jnp.transpose(a, (*range(n), n + 1, n, n + 2))
        return a.reshape(*lead, ny, nz)

    own = natural(state)
    k = natural(diffusivity)
    pos = lax.axis_index("gx").astype(jnp.int32).reshape(1)
    count = lax.axis_size("gy")
    segments = lax.axis_size("gx")
    chips = segments // 2
    starts = [sum(CHUNKS[:n]) for n in range(len(CHUNKS))]

    anywhere = pl.BlockSpec(memory_space=pl.ANY)
    hbm = pl.BlockSpec(memory_space=pltpu.HBM)
    up = [(i, (i + 1) % count) for i in range(count)]
    down = [((i + 1) % count, i) for i in range(count)]
    lefts, rights = [], []

    def send(n, *behind):
        piece = call(
            functools.partial(cut_kernel, starts[n], CHUNKS[n]),
            shape(comps, CHUNKS[n], *PLANE),
            [hbm] + [anywhere] * len(behind),
            [pltpu.SemaphoreType.DMA(())],
            16 * 1024 * 1024 if n else FIRST_ROOM,
        )(own, *behind)
        lefts.append(lax.ppermute(piece, "gy", up))
        rights.append(lax.ppermute(piece, "gy", down))

    send(0)
    pair = [(i, i ^ 1) for i in range(segments)]
    mine = call(summary_kernel, shape(SEG, *PLANE), [VMEM])(k)
    other = lax.ppermute(mine, "gx", pair)
    joined = call(pair_kernel, shape(SEG, *PLANE), [SMEM, VMEM, VMEM])(pos, mine, other)
    for n in range(1, len(CHUNKS)):
        send(n, joined)
    around = [
        lax.ppermute(joined, "gx", [((i + 2 * d) % segments, i) for i in range(segments)])
        for d in range(1, chips)
    ]
    table = shape(2, ROWS, *PLANE)
    r, ip, wip, wp, misc = call(
        coefficient_kernel,
        (table, table, table, table, shape(MISC, *PLANE)),
        [SMEM] + [VMEM] * 6,
    )(pos, k, mine, other, *around)

    ys = []
    carry = ()
    both = shape(2, comps, *PLANE)
    for n, (start, size) in enumerate(zip(starts, CHUNKS)):
        y, ends = call(
            functools.partial(explicit_kernel, start, size),
            (shape(comps, size, *PLANE), both),
            [VMEM] * (5 + len(carry)),
            [pltpu.VMEM((comps, 8, 8, 128), F32), pltpu.VMEM((comps, *PLANE), F32)],
        )(lefts[n], own, rights[n], r, wp, *carry)
        carry = (ends,)
        ys.append(y)

    other_ends = lax.ppermute(ends, "gx", pair)
    plane = shape(comps, *PLANE)
    chip_ends = call(chip_kernel, (plane,) * (chips - 1), [SMEM] + [VMEM] * 3)(pos, ends, other_ends, misc)
    flows = [
        lax.ppermute(chip_ends[d - 1], "gx", [(i, (i + 2 * d) % segments) for i in range(segments)])
        for d in range(1, chips)
    ]
    pieces = []
    for n in reversed(range(len(CHUNKS))):
        for high in range(CHUNKS[n], 0, -PIECE):
            pieces.append((n, max(high - PIECE, 0), high))
    result = pl.pallas_call(
        functools.partial(final_kernel, starts, pieces),
        out_shape=shape(comps, rows, *PLANE),
        in_specs=[SMEM] + [VMEM] * (8 + len(ys)),
        out_specs=anywhere,
        scratch_shapes=[
            pltpu.VMEM((comps, rows, *PLANE), F32),
            pltpu.SemaphoreType.DMA((len(pieces),)),
        ],
        compiler_params=pltpu.CompilerParams(vmem_limit_bytes=16 * 1024 * 1024),
    )(pos, other_ends, *flows, misc, r, ip, wip, *ys)
    return unnatural(result)


def solution(mesh):
    return jax.shard_map(
        body,
        mesh=mesh,
        in_specs=(P(None, "gx", "gy", None), P("gx", "gy", None)),
        out_specs=P(None, "gx", "gy", None),
        check_vma=False,
    )
```

```python
import functools

import jax
import jax.numpy as jnp
from jax import lax
from jax.experimental import pallas as pl
from jax.experimental.pallas import tpu as pltpu
from jax.sharding import PartitionSpec as P

diff_number = 4000.0
scalar_ratio = 1.4
step_size = 0.1


ROWS = 32
CHUNKS = (17, 9, 4, 2)
PIECE = 6
SCALES = (0.5 * diff_number, 0.5 * diff_number * scalar_ratio)
F32 = jnp.float32
VMEM = pl.BlockSpec(memory_space=pltpu.VMEM)
SMEM = pl.BlockSpec(memory_space=pltpu.SMEM)
PLANE = (32, 128)

SEG = 10
(W_UP, W_DOWN, R_UP, R_DOWN, RW_UP, RW_DOWN, AHEAD, _, _, BACK, _, _, ALPHA, BETA, BETAW) = range(0, 30, 2)
MISC = 30


def shape(*dims):
    return jax.ShapeDtypeStruct(dims, F32)


def call(kernel, outs, ins, scratch=(), room=16 * 1024 * 1024):
    return pl.pallas_call(
        kernel,
        out_shape=outs,
        in_specs=ins,
        out_specs=jax.tree.map(lambda _: VMEM, outs),
        scratch_shapes=list(scratch),
        compiler_params=pltpu.CompilerParams(vmem_limit_bytes=room),
    )


def summary_kernel(k_ref, out_ref):
    one = jnp.ones(PLANE, F32)
    zero = jnp.zeros(PLANE, F32)

    def step(i, carry):
        inv = 1.0 / (k_ref[i - 1] + k_ref[i])
        out = []
        for s in range(2):
            a, b, d, f = carry[4 * s : 4 * s + 4]
            q = inv * (1.0 / SCALES[s])
            d = q * a + d
            f = q * b + f
            out += [a + d, b + f, d, f]
        return tuple(out)

    final = lax.fori_loop(1, ROWS, step, (one, one, zero, one) * 2)
    for n in range(8):
        out_ref[n] = final[n]
    out_ref[8] = k_ref[0]
    out_ref[9] = k_ref[ROWS - 1]


def pair_kernel(pos_ref, mine_ref, other_ref, out_ref):
    right = pos_ref[0] % 2 == 1

    def lower(n):
        return jnp.where(right, other_ref[n], mine_ref[n])

    def upper(n):
        return jnp.where(right, mine_ref[n], other_ref[n])

    inv = 1.0 / (lower(9) + upper(8))
    for s in range(2):
        a, b, d, f = (lower(4 * s + n) for n in range(4))
        q = inv * (1.0 / SCALES[s])
        d = q * a + d
        f = q * b + f
        ua, ub, ud, uf = (upper(4 * s + n) for n in range(4))
        out_ref[4 * s] = ua * a + ub * d
        out_ref[4 * s + 1] = ua * b + ub * f
        out_ref[4 * s + 2] = ud * a + uf * d
        out_ref[4 * s + 3] = ud * b + uf * f
    out_ref[8] = lower(8)
    out_ref[9] = upper(9)


def coefficient_kernel(pos_ref, k_ref, mine_ref, other_ref, n1_ref, n2_ref, n3_ref, r_ref, ip_ref, wip_ref, wp_ref, misc_ref):
    position = pos_ref[0]
    right = position % 2 == 1
    chip = position // 2

    def lower(n):
        return jnp.where(right, other_ref[n], mine_ref[n])

    def upper(n):
        return jnp.where(right, mine_ref[n], other_ref[n])

    def series(scale, e, k_a, k_b):
        r = 1.0 / (1.0 + e / (scale * (k_a + k_b)))
        return r, e * r

    ahead_in, back_in = [], []
    last = []
    for s in range(2):
        scale = SCALES[s]

        def entries(get, flipped):
            a, b, d, f = (get(4 * s + n) for n in range(4))
            return (f, b, d, a) if flipped else (a, b, d, f)

        def through(get, flipped, g):
            a, b, d, f = entries(get, flipped)
            den = 1.0 / (d * g + f)
            return (a * g + b) * den, den

        def chain(far, mid, near, flipped, masks, k_own):
            tail, head = (8, 9) if flipped else (9, 8)
            e, _ = through(lambda n: far[n], flipped, scale * far[head])
            r3, g = series(scale, e, far[tail], mid[head])
            g = jnp.where(masks[2], g, scale * mid[head])
            e, den2 = through(lambda n: mid[n], flipped, g)
            r2, g = series(scale, e, mid[tail], near[head])
            g = jnp.where(masks[1], g, scale * near[head])
            e, den1 = through(lambda n: near[n], flipped, g)
            r1, g = series(scale, e, near[tail], k_own)
            g = jnp.where(masks[0], g, scale * k_own)
            w1 = jnp.where(masks[0], r1, 0.0)
            w2 = jnp.where(masks[1], r1 * r2 * den1, 0.0)
            w3 = jnp.where(masks[2], r1 * r2 * r3 * den1 * den2, 0.0)
            return g, e, (w1, w2, w3)

        left_masks = [chip >= n for n in (1, 2, 3)]
        right_masks = [chip <= n for n in (2, 1, 0)]
        g_left, _, ahead = chain(n1_ref, n2_ref, n3_ref, False, left_masks, lower(8))
        g_right, e_right, back = chain(n3_ref, n2_ref, n1_ref, True, right_masks, upper(9))
        e_mid, den_mid = through(lower, False, g_left)
        r_mid, g_mid = series(scale, e_mid, lower(9), upper(8))
        e_mid_b, den_mid_b = through(upper, True, g_right)
        r_mid_b, g_mid_b = series(scale, e_mid_b, lower(9), upper(8))
        _, den_upper = through(upper, False, g_mid)
        _, den_lower = through(lower, True, g_mid_b)
        misc_ref[W_UP + s] = r_mid * den_upper
        misc_ref[W_DOWN + s] = r_mid_b * den_lower
        misc_ref[R_UP + s] = r_mid
        misc_ref[R_DOWN + s] = r_mid_b
        misc_ref[RW_UP + s] = r_mid * den_mid
        misc_ref[RW_DOWN + s] = r_mid_b * den_mid_b
        for n in range(3):
            misc_ref[AHEAD + 2 * n + s] = ahead[n]
            misc_ref[BACK + 2 * n + s] = back[2 - n]
        ahead_in.append(1.0 + jnp.where(right, g_mid, g_left))
        back_in.append(1.0 + jnp.where(right, g_right, g_mid_b))
        k_next = jnp.where(right, n1_ref[8], upper(8))
        inner = jnp.where(position < 7, 1.0, 0.0)
        last.append((scale * (k_ref[ROWS - 1] + k_next * inner), inner, jnp.where(right, e_right, e_mid_b)))

    one = jnp.ones(PLANE, F32)

    def step(i, carry):
        e0, e1, w0, w1, b0, b1 = carry
        j = ROWS - 1 - i
        inv = 1.0 / (k_ref[i] + k_ref[i + 1])
        inv_b = 1.0 / (k_ref[j - 1] + k_ref[j])
        out_e, out_w, out_b = [], [], []
        for s, e, w, b in ((0, e0, w0, b0), (1, e1, w1, b1)):
            q = inv * (1.0 / SCALES[s])
            r = 1.0 / (1.0 + q * e)
            ip = r * q
            r_ref[s, i] = r
            ip_ref[s, i] = ip
            wip_ref[s, i] = w * ip
            out_e.append(1.0 + e * r)
            out_w.append(w * r)
            r_b = 1.0 / (1.0 + inv_b * (1.0 / SCALES[s]) * b)
            wp_ref[s, j] = r_b
            out_b.append(1.0 + b * r_b)
        return (*out_e, *out_w, *out_b)

    carry = lax.fori_loop(0, ROWS - 1, step, (*ahead_in, one, one, *back_in))
    for s in range(2):
        e, w = carry[s], carry[2 + s]
        c, inner, e_next = last[s]
        ip = 1.0 / (c + e)
        r = c * ip
        r_ref[s, ROWS - 1] = r
        ip_ref[s, ROWS - 1] = ip
        wip_ref[s, ROWS - 1] = w * ip
        inv = 1.0 / (c + e_next)
        den = 1.0 / (e * ip + r * e_next * inv)
        beta = inner * c * inv * ip * den
        misc_ref[ALPHA + s] = inner * den / c
        misc_ref[BETA + s] = beta
        misc_ref[BETAW + s] = beta * w
        wp_ref[s, 0] = one

    def spread(i, carry):
        out = []
        for s in range(2):
            w = carry[s] * wp_ref[s, i]
            wp_ref[s, i] = w
            out.append(w)
        return tuple(out)

    lax.fori_loop(1, ROWS, spread, (one, one))


def explicit_kernel(start, count, left_ref, own_ref, right_ref, r_ref, wp_ref, *refs):
    if start:
        before_ref, *refs = refs
    y_ref, after_ref, mid_ref, mixed_ref = refs
    lane = lax.broadcasted_iota(jnp.int32, (8, 128), 1)
    two_low = lane < 2
    top = lane >= 127

    def along_z(q):
        w = pltpu.roll(jnp.where(two_low, pltpu.roll(q, 7, 0), q), 126, 1) - q
        g = 8.0 * w - pltpu.roll(jnp.where(top, pltpu.roll(w, 1, 0), w), 1, 1)
        return pltpu.roll(jnp.where(top, pltpu.roll(g, 1, 0), g), 1, 1) - w

    def row(c, x, j):
        if j < 0:
            return left_ref[c, x, pl.ds(j + 4, 8, stride=4), :]
        if j < 4:
            return own_ref[c, start + x, pl.ds(j, 8, stride=4), :]
        return right_ref[c, x, pl.ds(j - 4, 8, stride=4), :]

    full = step_size / 12.0

    def step(x, carry):
        speed_y = [row(1, x, j) * full for j in range(-2, 6)]
        speed_z = [row(2, x, j) * full for j in range(-2, 6)]
        for c in range(4):
            q = [row(c, x, j) for j in range(-4, 8)]
            for n in range(8):
                dy = 8.0 * (q[n + 3] - q[n + 1]) - (q[n + 4] - q[n])
                mid_ref[c, n] = q[n + 2] - (speed_y[n] * dy + speed_z[n] * along_z(q[n + 2]))
        speed_y = [mid_ref[1, n] * (0.5 * full) for n in range(2, 6)]
        speed_z = [mid_ref[2, n] * (0.5 * full) for n in range(2, 6)]
        for c in range(4):
            m = [mid_ref[c, n] for n in range(8)]
            for n in range(4):
                dy = 8.0 * (m[n + 3] - m[n + 1]) - (m[n + 4] - m[n])
                value = 0.5 * (row(c, x, n) + m[n + 2]) - (speed_y[n] * dy + speed_z[n] * along_z(m[n + 2]))
                mixed_ref[c, pl.ds(n, 8, stride=4), :] = value
        before = jnp.maximum(start + x - 1, 0)
        for c in range(4):
            s = c // 3
            f = mixed_ref[c]
            y = f + r_ref[s, before] * after_ref[0, c]
            y_ref[c, x] = y
            after_ref[0, c] = y
            after_ref[1, c] = after_ref[1, c] + wp_ref[s, start + x] * f
        return carry

    if start:
        after_ref[...] = before_ref[...]
    else:
        after_ref[...] = jnp.zeros_like(after_ref)
    lax.fori_loop(0, count, step, 0)


def chip_kernel(pos_ref, own_ref, other_ref, misc_ref, *out_refs):
    right = pos_ref[0] % 2 == 1
    chip = pos_ref[0] // 2
    for c in range(4):
        s = c // 3
        own, other = (own_ref[0, c], own_ref[1, c]), (other_ref[0, c], other_ref[1, c])
        lower = [jnp.where(right, o, m) for m, o in zip(own, other)]
        upper = [jnp.where(right, m, o) for m, o in zip(own, other)]
        ahead = upper[0] + misc_ref[W_UP + s] * lower[0]
        back = lower[1] + misc_ref[W_DOWN + s] * upper[1]
        for d, out_ref in enumerate(out_refs, 1):
            out_ref[c] = jnp.where(chip + d < 4, ahead, back)


def final_kernel(starts, pieces, pos_ref, other_ref, a_ref, b_ref, c_ref, misc_ref, r_ref, ip_ref, wip_ref, *refs):
    y_refs, (out_ref, x_ref, sem) = refs[: len(CHUNKS)], refs[len(CHUNKS) :]
    right = pos_ref[0] % 2 == 1
    inflow, after = [], []
    for c in range(4):
        s = c // 3
        values = a_ref[c], b_ref[c], c_ref[c]
        ahead = sum(misc_ref[AHEAD + 2 * n + s] * values[n] for n in range(3))
        back = sum(misc_ref[BACK + 2 * n + s] * values[n] for n in range(3))
        near_ahead = misc_ref[R_UP + s] * other_ref[0, c] + misc_ref[RW_UP + s] * ahead
        near_back = misc_ref[R_DOWN + s] * other_ref[1, c] + misc_ref[RW_DOWN + s] * back
        ahead, back = jnp.where(right, near_ahead, ahead), jnp.where(right, back, near_back)
        inflow.append(ahead)
        after.append(misc_ref[ALPHA + s] * back + misc_ref[BETA + s] * y_refs[-1][c, CHUNKS[-1] - 1] + misc_ref[BETAW + s] * ahead)

    carry = tuple(after)
    copies = []
    for number, (n, low, high) in enumerate(pieces):

        def step(i, carry, n=n, high=high):
            x = high - 1 - i
            row = starts[n] + x
            out = []
            for c in range(4):
                s = c // 3
                value = y_refs[n][c, x] * ip_ref[s, row] + wip_ref[s, row] * inflow[c] + r_ref[s, row] * carry[c]
                x_ref[c, row] = value
                out.append(value)
            return tuple(out)

        carry = lax.fori_loop(0, high - low, step, carry)
        part = pl.ds(starts[n] + low, high - low)
        copy = pltpu.make_async_copy(x_ref.at[:, part], out_ref.at[:, part], sem.at[number])
        copy.start()
        copies.append(copy)
    for copy in copies:
        copy.wait()


def cut_kernel(start, count, whole_ref, *refs):
    out_ref, sem = refs[-2:]
    copy = pltpu.make_async_copy(whole_ref.at[:, pl.ds(start, count)], out_ref, sem)
    copy.start()
    copy.wait()


def body(state, diffusivity):
    comps, rows, ny, nz = state.shape
    tiles = nz // 128

    def natural(a):
        lead = a.shape[:-2]
        a = a.reshape(*lead, ny, tiles, 128)
        n = len(lead)
        a = jnp.transpose(a, (*range(n), n + 1, n, n + 2))
        return a.reshape(*lead, tiles * ny, 128)

    def unnatural(a):
        lead = a.shape[:-2]
        a = a.reshape(*lead, tiles, ny, 128)
        n = len(lead)
        a = jnp.transpose(a, (*range(n), n + 1, n, n + 2))
        return a.reshape(*lead, ny, nz)

    own = natural(state)
    k = natural(diffusivity)
    pos = lax.axis_index("gx").astype(jnp.int32).reshape(1)
    count = lax.axis_size("gy")
    segments = lax.axis_size("gx")
    chips = segments // 2
    starts = [sum(CHUNKS[:n]) for n in range(len(CHUNKS))]

    anywhere = pl.BlockSpec(memory_space=pl.ANY)
    hbm = pl.BlockSpec(memory_space=pltpu.HBM)
    up = [(i, (i + 1) % count) for i in range(count)]
    down = [((i + 1) % count, i) for i in range(count)]
    lefts, rights = [], []

    def send(n, *behind):
        piece = call(
            functools.partial(cut_kernel, starts[n], CHUNKS[n]),
            shape(comps, CHUNKS[n], *PLANE),
            [hbm] + [anywhere] * len(behind),
            [pltpu.SemaphoreType.DMA(())],
        )(own if n else pltpu.with_memory_space_constraint(own, pltpu.HBM), *behind)
        lefts.append(lax.ppermute(piece, "gy", up))
        rights.append(lax.ppermute(piece, "gy", down))

    send(0)
    pair = [(i, i ^ 1) for i in range(segments)]
    mine = call(summary_kernel, shape(SEG, *PLANE), [VMEM])(k)
    other = lax.ppermute(mine, "gx", pair)
    joined = call(pair_kernel, shape(SEG, *PLANE), [SMEM, VMEM, VMEM])(pos, mine, other)
    for n in range(1, len(CHUNKS)):
        send(n, joined)
    around = [
        lax.ppermute(joined, "gx", [((i + 2 * d) % segments, i) for i in range(segments)])
        for d in range(1, chips)
    ]
    table = shape(2, ROWS, *PLANE)
    r, ip, wip, wp, misc = call(
        coefficient_kernel,
        (table, table, table, table, shape(MISC, *PLANE)),
        [SMEM] + [VMEM] * 6,
    )(pos, k, mine, other, *around)

    ys = []
    carry = ()
    both = shape(2, comps, *PLANE)
    for n, (start, size) in enumerate(zip(starts, CHUNKS)):
        y, ends = call(
            functools.partial(explicit_kernel, start, size),
            (shape(comps, size, *PLANE), both),
            [VMEM] * (5 + len(carry)),
            [pltpu.VMEM((comps, 8, 8, 128), F32), pltpu.VMEM((comps, *PLANE), F32)],
        )(lefts[n], own, rights[n], r, wp, *carry)
        carry = (ends,)
        ys.append(y)

    other_ends = lax.ppermute(ends, "gx", pair)
    plane = shape(comps, *PLANE)
    chip_ends = call(chip_kernel, (plane,) * (chips - 1), [SMEM] + [VMEM] * 3)(pos, ends, other_ends, misc)
    flows = [
        lax.ppermute(chip_ends[d - 1], "gx", [(i, (i + 2 * d) % segments) for i in range(segments)])
        for d in range(1, chips)
    ]
    pieces = []
    for n in reversed(range(len(CHUNKS))):
        for high in range(CHUNKS[n], 0, -PIECE):
            pieces.append((n, max(high - PIECE, 0), high))
    result = pl.pallas_call(
        functools.partial(final_kernel, starts, pieces),
        out_shape=shape(comps, rows, *PLANE),
        in_specs=[SMEM] + [VMEM] * (8 + len(ys)),
        out_specs=anywhere,
        scratch_shapes=[
            pltpu.VMEM((comps, rows, *PLANE), F32),
            pltpu.SemaphoreType.DMA((len(pieces),)),
        ],
        compiler_params=pltpu.CompilerParams(vmem_limit_bytes=16 * 1024 * 1024),
    )(pos, other_ends, *flows, misc, r, ip, wip, *ys)
    return unnatural(result)


def solution(mesh):
    return jax.shard_map(
        body,
        mesh=mesh,
        in_specs=(P(None, "gx", "gy", None), P("gx", "gy", None)),
        out_specs=P(None, "gx", "gy", None),
        check_vma=False,
    )
```
